512 devices in a mesh: feat: 128 (over x, y, z_hi), rows: 4 (over z_lo, core).
Axes of the slice: x: 4, y: 8, z: 8 (z_hi: 4, z_lo: 2; z = z_hi * 2 + z_lo), core: 2. Of those that a mesh axis runs over, the one named last changes fastest.
Arguments:
- binned: int32 [8192, 8192], P('rows', 'feat'), may hold values from 0 to 255
- node_of: int32 [8192], P('rows'), may hold values from 0 to 31
- margin: float32 [8192], P('rows'), may hold values from -6 to 6
- labels: float32 [8192], P('rows'), may hold values from 0 to 1
- split_feature: int32 [32], replicated, may hold values from 0 to 8191
- split_bin: int32 [32], replicated, may hold values from 0 to 255
Outputs:
- histogram: float32 [32, 2, 8192, 256], P('rows', None, 'feat')
- margin_out: float32 [8192], P('rows')
- child_out: int32 [8192], P('rows')
- grad_out: float32 [2, 8192], P(None, 'rows')
The draws below stay inside these ranges and needn't reach their ends.
All inputs are finite; a program needn't handle non-finite values.
Results may differ from the reference program's by a relative error of at most 0.0045.
Values may be sent and summed in bfloat16 or wider, within the bound.
No kernel may reach another device: no remote copies, remote signals or barrier semaphores. Data moves between devices by JAX's collectives and lax.ppermute only.
A program may use at most 64 MiB of HBM per device.

```python
import jax
import jax.numpy as jnp
from jax import lax

F = 8192
BINS = 256
NODES = 32
ROW_DEV = 2048
ROWS = 8192
N_ROWS = 4


def with_ends(array, stream_key, low, largest):
    shape = array.shape
    index_at = [jax.random.randint(jax.random.fold_in(stream_key, axis), (), 0, shape[axis]) for axis in range(len(shape))]
    array = array.at[tuple(index_at)].set(low)
    longest = shape.index(max(shape))
    index_at[longest] = (index_at[longest] + 1) % shape[longest]
    return array.at[tuple(index_at)].set(largest)


def levels(own_key, extent, pieces, least, largest):
    level = 1.0
    for dim, shards_of in pieces:
        steps = jax.random.uniform(jax.random.fold_in(jax.random.fold_in(own_key, 6), dim), (shards_of,), jnp.float32, least / len(pieces), largest / len(pieces))
        level = level * jnp.repeat(jnp.exp(steps), extent[dim] // shards_of).reshape((-1,) + (1,) * (len(extent) - 1 - dim))
    return level


def bell_draw(rng, dims, deviation, limit, split=(), held_as=jnp.bfloat16):
    array = jax.random.normal(rng, dims, jnp.float32) * deviation
    if len(split) > 0:
        array = levels(rng, dims, split, -0.22, 0.18) * array
    return jnp.clip(array, min=-limit, max=limit).astype(held_as)


def setup_inputs(seed: int = 0) -> dict:
    keys = jax.random.split(jax.random.key(seed), 7)
    return {
        "binned": with_ends(jax.random.randint(keys[0], (ROWS, F), 0, BINS), jax.random.fold_in(keys[0], 1), 0, BINS - 1).astype(jnp.int32),
        "node_of": with_ends(jax.random.randint(keys[1], (ROWS,), 0, NODES), jax.random.fold_in(keys[1], 1), 0, NODES - 1).astype(jnp.int32),
        "margin": bell_draw(keys[2], (ROWS,), 1.0, 6.0, ((0, 4),), jnp.float32),
        "labels": jnp.clip(1.0 * jax.random.uniform(keys[3], (ROWS,), jnp.float32) ** levels(keys[3], (ROWS,), ((0, 4),), -0.2, 0.2), 0.0, 1.0),
        "split_feature": with_ends(jax.random.randint(keys[4], (NODES,), 0, F), jax.random.fold_in(keys[4], 1), 0, F - 1).astype(jnp.int32),
        "split_bin": with_ends(jax.random.randint(keys[5], (NODES,), 0, BINS), jax.random.fold_in(keys[5], 1), 0, BINS - 1).astype(jnp.int32),
    }


def leaf_table(selected, split_rows):
    below = (jnp.arange(selected.shape[2])[None, :] <= split_rows[:, None]).astype(jnp.float32)
    left = jnp.sum(selected * below[:, None, :], axis=2)
    whole = jnp.sum(selected, axis=2)
    return jnp.concatenate([left, whole], axis=1)


def reference(binned, node_of, margin, labels, split_feature, split_bin):
    probability = jax.nn.sigmoid(margin)
    gradient = (probability - labels).astype(jnp.bfloat16)
    hessian = (probability * (1.0 - probability)).astype(jnp.bfloat16)
    gradient = lax.optimization_barrier(gradient).astype(jnp.float32)
    hessian = lax.optimization_barrier(hessian).astype(jnp.float32)
    cells = NODES * 2 * F * BINS
    total = jnp.zeros((cells,), jnp.float32)
    feature_ids = jnp.arange(F, dtype=jnp.int32)
    for shard in range(N_ROWS):
        lower = shard * ROW_DEV
        block_bins = binned[lower:lower + ROW_DEV]
        block_nodes = node_of[lower:lower + ROW_DEV]
        for column, values in enumerate((gradient, hessian)):
            index = ((block_nodes[:, None] * 2 + column) * F + feature_ids[None, :]) * BINS + block_bins
            spread = jnp.broadcast_to(values[lower:lower + ROW_DEV][:, None], block_bins.shape)
            part = jax.ops.segment_sum(spread.reshape(-1), index.reshape(-1).astype(jnp.int32), num_segments=cells)
            part = lax.optimization_barrier(part.astype(jnp.bfloat16))
            total = total + part.astype(jnp.float32)
    histogram = total.reshape(NODES, 2, F, BINS)
    selected = histogram[jnp.arange(NODES), :, split_feature, :]
    table = leaf_table(selected, split_bin)
    leaf_left = -table[:, 0] / (table[:, 1] + 1.0)
    leaf_right = -(table[:, 2] - table[:, 0]) / (table[:, 3] - table[:, 1] + 1.0)
    row_feature = split_feature[node_of]
    row_value = jnp.take_along_axis(binned, row_feature[:, None], axis=1)[:, 0]
    go_right = (row_value > split_bin[node_of]).astype(jnp.int32)
    child_out = 2 * node_of + go_right
    margin_out = margin + jnp.where(go_right == 1, leaf_right[node_of], leaf_left[node_of])
    fresh = jax.nn.sigmoid(margin_out)
    grad_out = jnp.stack([fresh - labels, fresh * (1.0 - fresh)], axis=0)
    return histogram, margin_out, child_out, grad_out
```

```python
import jax
import jax.numpy as jnp
from jax import lax
from jax.experimental import pallas as pl
from jax.experimental.pallas import tpu as pltpu
from jax.sharding import Mesh
from jax.sharding import PartitionSpec as P

BINS = 256
NODES = 32
ROWS = 2048
FEATS = 64
TILE = 256
FEAT_AXES = ("x", "y", "zh")
ROW_AXES = ("zl", "core")
PLANE = ("x", "y")
LINE = ("zh", "zl", "core")
F32 = jnp.float32
BF16 = jnp.bfloat16
VMEM = pl.BlockSpec(memory_space=pltpu.VMEM)


def iota(shape, dim):
    return lax.broadcasted_iota(jnp.int32, shape, dim)


def cost(flops, moved):
    return pl.CostEstimate(flops=flops, bytes_accessed=moved, transcendentals=0)


def contract_last(a, b):
    return lax.dot_general(a, b, (((1,), (1,)), ((), ())), preferred_element_type=F32)


def bin_hot(row, bins):
    col = jnp.broadcast_to(row, (16, TILE)).astype(BF16)
    col = jnp.concatenate([col] * (BINS // 16), axis=0)
    return jnp.where(bins == col, BF16(1), BF16(0))


def bin_sums(weights_ref, row_of, bins):
    total = None
    for k in range(ROWS // TILE):
        piece = contract_last(weights_ref[:, k * TILE : (k + 1) * TILE], bin_hot(row_of(k), bins))
        total = piece if total is None else total + piece
    return total


def bins_tile():
    return iota((BINS, TILE), 0).astype(F32).astype(BF16)


def stage_kernel(binned, node, margin, labels, feature, cut, weights, columns, pay, chosen):
    here = lax.axis_index("zl") * 2 + lax.axis_index("core")
    feat_start = (
        (lax.axis_index("x") * 8 + lax.axis_index("y")) * 4 + lax.axis_index("zh")
    ) * FEATS
    probability = jax.nn.sigmoid(margin[...])
    gradient = probability - labels[...]
    hessian = probability * (1.0 - probability)
    q = iota((2 * NODES, 1), 0)
    block = q // 16
    block = jnp.where(block < 2, 2 * block + 1, 2 * block - 4)
    node_q = (block * 8 + (q % 16) // 2) ^ (here * 8)
    channel = q % 2
    values = jnp.where(channel == 0, gradient, hessian)
    weights[...] = jnp.where(node[...] == node_q, values, 0.0).astype(BF16)
    local = feature[...] - feat_start
    diagonal = iota((NODES, NODES), 0) == iota((NODES, NODES), 1)
    local_n = jnp.sum(jnp.where(diagonal, local, 0), axis=1, keepdims=True)
    cut_n = jnp.sum(jnp.where(diagonal, cut[...], 0), axis=1, keepdims=True)
    owned_n = (local_n >= 0) & (local_n < FEATS)
    picker = jnp.where(
        iota((FEATS, FEATS), 0) == iota((FEATS, FEATS), 1), 1.0, 0.0
    ).astype(BF16)
    chooser = jnp.where(iota((NODES, FEATS), 1) == local_n, 1.0, 0.0).astype(BF16)
    table_bf = binned[...].astype(F32).astype(BF16)
    columns[...] = contract_last(picker, table_bf)
    split_values = contract_last(chooser, table_bf)
    hot = node[...] == iota((NODES, ROWS), 0)
    value = jnp.sum(jnp.where(hot, split_values, 0.0), axis=0, keepdims=True)
    owned = jnp.sum(jnp.where(hot & owned_n, 1.0, 0.0), axis=0, keepdims=True)
    row_cut = jnp.sum(jnp.where(hot, cut_n.astype(F32), 0.0), axis=0, keepdims=True)
    right = jnp.where(value > row_cut, owned, 0.0)
    chosen[...] = jnp.where(owned > 0.5, value, -1.0)
    bins = bins_tile()
    sums = bin_sums(weights, lambda k: chosen[:, k * TILE : (k + 1) * TILE], bins)
    sums = sums.astype(BF16).astype(F32)
    cut_q = jnp.sum(
        jnp.where(iota((2 * NODES, NODES), 1) == node_q, cut[...], 0), axis=1, keepdims=True
    )
    below = iota((2 * NODES, BINS), 1) <= cut_q
    left = jnp.sum(jnp.where(below, sums, 0.0), axis=1, keepdims=True)
    whole = jnp.sum(sums, axis=1, keepdims=True)
    lane = iota((2 * NODES, 128), 1)
    slot = 2 * node_q + channel
    entries = jnp.where(lane == slot, left, 0.0) + jnp.where(lane == slot + 64, whole, 0.0)
    pay[...] = jnp.zeros((16, 128), F32)
    pay[8:9, :] = jnp.sum(entries, axis=0, keepdims=True)
    half = ROWS // 2
    for i in range(8):
        pay[i : i + 1, :] = (
            right[:, i * 128 : (i + 1) * 128]
            + 2.0 * right[:, half + i * 128 : half + (i + 1) * 128]
        )


def stage(binned, node, margin, labels, feature, cut):
    return pl.pallas_call(
        stage_kernel,
        out_shape=(
            jax.ShapeDtypeStruct((2 * NODES, ROWS), BF16),
            jax.ShapeDtypeStruct((FEATS, ROWS), F32),
            jax.ShapeDtypeStruct((16, 128), F32),
        ),
        in_specs=[VMEM] * 6,
        out_specs=[VMEM] * 3,
        scratch_shapes=[pltpu.VMEM((1, ROWS), F32)],
        name="stage",
        cost_estimate=cost(2 * 96 * ROWS * FEATS, 3 << 20),
    )(binned, node, margin, labels, feature, cut)


def histogram_kernel(weights, columns, send, keep):
    bins = bins_tile()

    def feature(f, carry):
        sums = bin_sums(
            weights, lambda k: columns[pl.ds(f, 1), k * TILE : (k + 1) * TILE], bins
        ).astype(BF16)
        send[f] = sums[:NODES]
        keep[f] = sums[NODES:]
        return carry

    lax.fori_loop(0, FEATS, feature, 0, unroll=4)


def histograms(weights, columns):
    half = jax.ShapeDtypeStruct((FEATS, NODES, BINS), BF16)
    return pl.pallas_call(
        histogram_kernel,
        out_shape=(half, half),
        in_specs=[VMEM] * 2,
        out_specs=[VMEM] * 2,
        name="histograms",
        cost_estimate=cost(2 * 64 * ROWS * FEATS * BINS, 3 << 20),
    )(weights, columns)


def chip_sum_kernel(keep, arrived, own, send):
    for f in range(0, FEATS, 8):
        total = keep[f : f + 8].astype(F32) + arrived[f : f + 8].astype(F32)
        own[f : f + 8] = total[:, :16]
        send[f : f + 8] = total[:, 16:].astype(BF16)


def chip_sum(keep, arrived):
    return pl.pallas_call(
        chip_sum_kernel,
        out_shape=(
            jax.ShapeDtypeStruct((FEATS, 16, BINS), F32),
            jax.ShapeDtypeStruct((FEATS, 16, BINS), BF16),
        ),
        in_specs=[VMEM] * 2,
        out_specs=[VMEM] * 2,
        name="chip_sum",
        cost_estimate=cost(FEATS * 32 * BINS, 3 << 20),
    )(keep, arrived)


def finish_kernel(
    own, arrived, parts, node, margin, labels, histogram, margin_out, child_out, grad_out, total
):
    for f in range(0, FEATS, 8):
        piece = (own[f : f + 8] + arrived[f : f + 8].astype(F32)).reshape(128, BINS)
        for h in range(2):
            total[h, f * 16 : (f + 8) * 16, :] = piece[:, h * 128 : (h + 1) * 128]
    for q in range(16):
        for h in range(2):
            histogram[q, :, h * 128 : (h + 1) * 128] = total[h, pl.ds(q, FEATS, stride=16), :]
    here = lax.axis_index("zl") * 2 + lax.axis_index("core")
    codes = parts[here, 0:8, :]
    for z in range(1, 4):
        codes = codes + parts[4 * z + here, 0:8, :]
    table = parts[0, 8:16, :]
    for m in range(1, 16):
        table = table + parts[m, 8:16, :]
    table = jnp.broadcast_to(table[0:1, :], (8, 128))
    rest = pltpu.roll(table, 64, 1) - table
    leaf_left = -table / (pltpu.roll(table, 127, 1) + 1.0)
    leaf_right = -rest / (pltpu.roll(rest, 127, 1) + 1.0)
    high = jnp.where(codes > 1.5, 1.0, 0.0)
    go_right = jnp.concatenate([codes - 2.0 * high, high], axis=0) > 0.5
    node_here = node[...]
    shift = jnp.zeros((16, 128), F32)
    for n in range(NODES):
        step = jnp.where(
            go_right,
            jnp.broadcast_to(leaf_right[0:1, 2 * n : 2 * n + 1], (16, 128)),
            jnp.broadcast_to(leaf_left[0:1, 2 * n : 2 * n + 1], (16, 128)),
        )
        shift = jnp.where(node_here == n, step, shift)
    moved = margin[...] + shift
    margin_out[...] = moved
    child_out[...] = 2 * node_here + jnp.where(go_right, 1, 0)
    fresh = jax.nn.sigmoid(moved)
    slope = fresh - labels[...]
    curve = fresh * (1.0 - fresh)
    for i in range(16):
        grad_out[0:1, i * 128 : (i + 1) * 128] = slope[i : i + 1, :]
        grad_out[1:2, i * 128 : (i + 1) * 128] = curve[i : i + 1, :]


def finish(own, arrived, parts, node, margin, labels):
    return pl.pallas_call(
        finish_kernel,
        out_shape=(
            jax.ShapeDtypeStruct((16, FEATS, BINS), F32),
            jax.ShapeDtypeStruct((16, 128), F32),
            jax.ShapeDtypeStruct((16, 128), jnp.int32),
            jax.ShapeDtypeStruct((2, ROWS), F32),
        ),
        in_specs=[VMEM] * 6,
        out_specs=[VMEM] * 4,
        scratch_shapes=[pltpu.VMEM((2, FEATS * 16, 128), F32)],
        name="finish",
        cost_estimate=cost(FEATS * 16 * BINS, 3 << 20),
    )(own, arrived, parts, node, margin, labels)


def share(part, axes, count):
    spread = jnp.broadcast_to(part[None], (count,) + part.shape)
    return lax.all_to_all(spread, axes, 0, 0, tiled=True)


def on_device(binned, node_of, margin, labels, split_feature, split_bin):
    swap = [(0, 1), (1, 0)]
    weights, columns, pay = stage(
        binned,
        node_of.reshape(1, ROWS),
        margin.reshape(1, ROWS),
        labels.reshape(1, ROWS),
        split_feature.reshape(1, NODES),
        split_bin.reshape(1, NODES),
    )
    send, keep = histograms(weights, columns)
    own, send_line = chip_sum(keep, lax.ppermute(send, "core", swap))
    arrived = lax.ppermute(send_line, "zl", swap)
    plane = jnp.sum(share(pay, PLANE, 32), axis=0)
    parts = share(plane, LINE, 16)
    histogram, margin_out, child_out, grad_out = finish(
        own,
        arrived,
        parts,
        node_of.reshape(16, 128),
        margin.reshape(16, 128),
        labels.reshape(16, 128),
    )
    return (
        histogram.reshape(8, 2, FEATS, BINS),
        margin_out.reshape(ROWS),
        child_out.reshape(ROWS),
        grad_out,
    )


def solution(mesh):
    fine = Mesh(mesh.devices.reshape(4, 8, 4, 2, 2), ("x", "y", "zh", "zl", "core"))
    rows = P(ROW_AXES)
    in_specs = (P(ROW_AXES, FEAT_AXES), rows, rows, rows, P(), P())
    out_specs = (P(ROW_AXES, None, FEAT_AXES, None), rows, rows, P(None, ROW_AXES))
    return jax.shard_map(
        on_device, mesh=fine, in_specs=in_specs, out_specs=out_specs, check_vma=False
    )
```

```python
import jax
import jax.numpy as jnp
from jax import lax
from jax.experimental import pallas as pl
from jax.experimental.pallas import tpu as pltpu
from jax.sharding import Mesh
from jax.sharding import PartitionSpec as P

BINS = 256
NODES = 32
ROWS = 2048
FEATS = 64
TILE = 256
FEAT_AXES = ("x", "y", "zh")
ROW_AXES = ("zl", "core")
PLANE = ("x", "y")
LINE = ("zh", "zl", "core")
F32 = jnp.float32
BF16 = jnp.bfloat16
I16 = jnp.int16
LIMIT = pltpu.CompilerParams(vmem_limit_bytes=16 << 20)
VMEM = pl.BlockSpec(memory_space=pltpu.VMEM)


def iota(shape, dim):
    return lax.broadcasted_iota(jnp.int32, shape, dim)


def cost(flops, moved):
    return pl.CostEstimate(flops=flops, bytes_accessed=moved, transcendentals=0)


def contract_last(a, b):
    return lax.dot_general(a, b, (((1,), (1,)), ((), ())), preferred_element_type=F32)


def bin_sums(weights, row_of):
    low_ids = iota((BINS // 2, TILE), 0).astype(I16)
    one, zero = BF16(1), BF16(0)
    total = None
    for k in range(ROWS // TILE):
        row = jnp.broadcast_to(row_of(k), (16, TILE))
        low = jnp.concatenate([(row & 127).astype(I16)] * 8, axis=0)
        high = jnp.concatenate([(row >> 7).astype(I16)] * 4, axis=0)
        tile = weights[:, k * TILE : (k + 1) * TILE]
        split = [jnp.where(high == h, tile, zero) for h in range(2)]
        hot = jnp.where(low_ids == low, one, zero)
        piece = contract_last(jnp.concatenate(split, axis=0), hot)
        total = piece if total is None else total + piece
    return total


def stage_kernel(columns, node, margin, labels, feature, cut, weights, pay, chosen):
    here = lax.axis_index("zl") * 2 + lax.axis_index("core")
    feat_start = (
        (lax.axis_index("x") * 8 + lax.axis_index("y")) * 4 + lax.axis_index("zh")
    ) * FEATS
    probability = jax.nn.sigmoid(margin[...])
    gradient = probability - labels[...]
    hessian = probability * (1.0 - probability)
    q = iota((2 * NODES, 1), 0)
    block = q // 16
    block = jnp.where(block < 2, 2 * block + 1, 2 * block - 4)
    node_q = (block * 8 + (q % 16) // 2) ^ (here * 8)
    channel = q % 2
    values = jnp.where(channel == 0, gradient, hessian)
    weights[...] = jnp.where(node[...] == node_q, values, 0.0).astype(BF16)
    local = feature[...] - feat_start
    diagonal = iota((NODES, NODES), 0) == iota((NODES, NODES), 1)
    local_n = jnp.sum(jnp.where(diagonal, local, 0), axis=1, keepdims=True)
    cut_n = jnp.sum(jnp.where(diagonal, cut[...], 0), axis=1, keepdims=True)
    owned_n = (local_n >= 0) & (local_n < FEATS)
    chooser = jnp.where(iota((NODES, FEATS), 1) == local_n, 1.0, 0.0).astype(BF16)
    split_values = jnp.dot(
        chooser, columns[...].astype(F32).astype(BF16), preferred_element_type=F32
    )
    hot = node[...] == iota((NODES, ROWS), 0)
    value = jnp.sum(jnp.where(hot, split_values, 0.0), axis=0, keepdims=True)
    owned = jnp.sum(jnp.where(hot & owned_n, 1.0, 0.0), axis=0, keepdims=True)
    row_cut = jnp.sum(jnp.where(hot, cut_n.astype(F32), 0.0), axis=0, keepdims=True)
    right = jnp.where(value > row_cut, owned, 0.0)
    chosen[...] = jnp.where(owned > 0.5, value, -1.0).astype(jnp.int32)
    sums = bin_sums(weights, lambda k: chosen[:, k * TILE : (k + 1) * TILE])
    sums = jnp.concatenate([sums[:64], sums[64:]], axis=1).astype(BF16).astype(F32)
    cut_q = jnp.sum(
        jnp.where(iota((2 * NODES, NODES), 1) == node_q, cut[...], 0), axis=1, keepdims=True
    )
    below = iota((2 * NODES, BINS), 1) <= cut_q
    left = jnp.sum(jnp.where(below, sums, 0.0), axis=1, keepdims=True)
    whole = jnp.sum(sums, axis=1, keepdims=True)
    lane = iota((2 * NODES, 128), 1)
    slot = 2 * node_q + channel
    entries = jnp.where(lane == slot, left, 0.0) + jnp.where(lane == slot + 64, whole, 0.0)
    pay[...] = jnp.zeros((16, 128), F32)
    pay[8:9, :] = jnp.sum(entries, axis=0, keepdims=True)
    half = ROWS // 2
    for i in range(8):
        pay[i : i + 1, :] = (
            right[:, i * 128 : (i + 1) * 128]
            + 2.0 * right[:, half + i * 128 : half + (i + 1) * 128]
        )


def stage(columns, node, margin, labels, feature, cut):
    return pl.pallas_call(
        stage_kernel,
        out_shape=(
            pltpu.VMEM((2 * NODES, ROWS), BF16),
            pltpu.VMEM((16, 128), F32),
        ),
        in_specs=[VMEM] * 6,
        out_specs=[VMEM] * 2,
        scratch_shapes=[pltpu.VMEM((1, ROWS), jnp.int32)],
        name="stage",
        compiler_params=LIMIT,
        cost_estimate=cost(2 * 96 * ROWS * FEATS, 3 << 20),
    )(columns, node, margin, labels, feature, cut)


def histogram_kernel(weights, columns, send, keep):
    def feature(f, carry):
        sums = bin_sums(
            weights, lambda k: columns[pl.ds(f, 1), k * TILE : (k + 1) * TILE]
        ).astype(BF16)
        for h in range(2):
            span = slice(h * 128, (h + 1) * 128)
            send[f, :, span] = sums[64 * h : 64 * h + NODES]
            keep[f, :, span] = sums[64 * h + NODES : 64 * h + 64]
        return carry

    lax.fori_loop(0, FEATS, feature, 0, unroll=8)


def histograms(weights, columns):
    half = pltpu.VMEM((FEATS, NODES, BINS), BF16)
    return pl.pallas_call(
        histogram_kernel,
        out_shape=(half, half),
        in_specs=[VMEM] * 2,
        out_specs=[VMEM] * 2,
        name="histograms",
        compiler_params=LIMIT,
        cost_estimate=cost(2 * 64 * ROWS * FEATS * BINS, 3 << 20),
    )(weights, columns)


def chip_sum_kernel(keep, arrived, own, send):
    for f in range(0, FEATS, 8):
        total = keep[f : f + 8].astype(F32) + arrived[f : f + 8].astype(F32)
        own[f : f + 8] = total[:, :16]
        send[f : f + 8] = total[:, 16:].astype(BF16)


def chip_sum(keep, arrived):
    return pl.pallas_call(
        chip_sum_kernel,
        out_shape=(
            pltpu.VMEM((FEATS, 16, BINS), F32),
            pltpu.VMEM((FEATS, 16, BINS), BF16),
        ),
        in_specs=[VMEM] * 2,
        out_specs=[VMEM] * 2,
        name="chip_sum",
        compiler_params=LIMIT,
        cost_estimate=cost(FEATS * 32 * BINS, 3 << 20),
    )(keep, arrived)


def finish_kernel(
    own, arrived, parts, node, margin, labels, histogram, margin_out, child_out, grad_out, total
):
    for f in range(0, FEATS, 8):
        piece = (own[f : f + 8] + arrived[f : f + 8].astype(F32)).reshape(128, BINS)
        for h in range(2):
            total[h, f * 16 : (f + 8) * 16, :] = piece[:, h * 128 : (h + 1) * 128]
    for q in range(16):
        for h in range(2):
            histogram[q, :, h * 128 : (h + 1) * 128] = total[h, pl.ds(q, FEATS, stride=16), :]
    here = lax.axis_index("zl") * 2 + lax.axis_index("core")
    codes = parts[here, 0:8, :]
    for z in range(1, 4):
        codes = codes + parts[4 * z + here, 0:8, :]
    table = parts[0, 8:16, :]
    for m in range(1, 16):
        table = table + parts[m, 8:16, :]
    table = jnp.broadcast_to(table[0:1, :], (8, 128))
    rest = pltpu.roll(table, 64, 1) - table
    leaf_left = -table / (pltpu.roll(table, 127, 1) + 1.0)
    leaf_right = -rest / (pltpu.roll(rest, 127, 1) + 1.0)
    high = jnp.where(codes > 1.5, 1.0, 0.0)
    go_right = jnp.concatenate([codes - 2.0 * high, high], axis=0) > 0.5
    node_here = node[...]
    shift = jnp.zeros((16, 128), F32)
    for n in range(NODES):
        step = jnp.where(
            go_right,
            jnp.broadcast_to(leaf_right[0:1, 2 * n : 2 * n + 1], (16, 128)),
            jnp.broadcast_to(leaf_left[0:1, 2 * n : 2 * n + 1], (16, 128)),
        )
        shift = jnp.where(node_here == n, step, shift)
    moved = margin[...] + shift
    margin_out[...] = moved
    child_out[...] = 2 * node_here + jnp.where(go_right, 1, 0)
    fresh = jax.nn.sigmoid(moved)
    slope = fresh - labels[...]
    curve = fresh * (1.0 - fresh)
    for i in range(16):
        grad_out[0:1, i * 128 : (i + 1) * 128] = slope[i : i + 1, :]
        grad_out[1:2, i * 128 : (i + 1) * 128] = curve[i : i + 1, :]


def finish(own, arrived, parts, node, margin, labels):
    return pl.pallas_call(
        finish_kernel,
        out_shape=(
            jax.ShapeDtypeStruct((16, FEATS, BINS), F32),
            jax.ShapeDtypeStruct((16, 128), F32),
            jax.ShapeDtypeStruct((16, 128), jnp.int32),
            jax.ShapeDtypeStruct((2, ROWS), F32),
        ),
        in_specs=[VMEM] * 6,
        out_specs=[VMEM] * 4,
        scratch_shapes=[pltpu.VMEM((2, FEATS * 16, 128), F32)],
        name="finish",
        compiler_params=LIMIT,
        cost_estimate=cost(FEATS * 16 * BINS, 3 << 20),
    )(own, arrived, parts, node, margin, labels)


def share(part, axes, count):
    spread = jnp.broadcast_to(part[None], (count,) + part.shape)
    return lax.all_to_all(spread, axes, 0, 0, tiled=True)


def near(array):
    return pltpu.with_memory_space_constraint(array, pltpu.VMEM)


def on_device(binned, node_of, margin, labels, split_feature, split_bin):
    swap = [(0, 1), (1, 0)]
    columns = binned.T
    weights, pay = stage(
        columns,
        node_of.reshape(1, ROWS),
        margin.reshape(1, ROWS),
        labels.reshape(1, ROWS),
        split_feature.reshape(1, NODES),
        split_bin.reshape(1, NODES),
    )
    plane = share(pay, PLANE, 32)
    send, keep = histograms(near(weights), columns)
    parts = share(jnp.sum(plane, axis=0), LINE, 16)
    arrived = lax.ppermute(send, "core", swap)
    own, send_line = chip_sum(near(keep), near(arrived))
    arrived = lax.ppermute(send_line, "zl", swap)
    own, arrived, parts = near(own), near(arrived), near(parts)
    histogram, margin_out, child_out, grad_out = finish(
        own,
        arrived,
        parts,
        node_of.reshape(16, 128),
        margin.reshape(16, 128),
        labels.reshape(16, 128),
    )
    return (
        histogram.reshape(8, 2, FEATS, BINS),
        margin_out.reshape(ROWS),
        child_out.reshape(ROWS),
        grad_out,
    )


def solution(mesh):
    fine = Mesh(mesh.devices.reshape(4, 8, 4, 2, 2), ("x", "y", "zh", "zl", "core"))
    rows = P(ROW_AXES)
    in_specs = (P(ROW_AXES, FEAT_AXES), rows, rows, rows, P(), P())
    out_specs = (P(ROW_AXES, None, FEAT_AXES, None), rows, rows, P(None, ROW_AXES))

    return jax.shard_map(
        on_device, mesh=fine, in_specs=in_specs, out_specs=out_specs, check_vma=False
    )
```

```python
import jax
import jax.numpy as jnp
from jax import lax
from jax.experimental import pallas as pl
from jax.experimental.pallas import tpu as pltpu
from jax.sharding import Mesh
from jax.sharding import PartitionSpec as P

BINS = 256
NODES = 32
ROWS = 2048
FEATS = 64
TILE = 256
FEAT_AXES = ("x", "y", "zh")
ROW_AXES = ("zl", "core")
PLANE = ("x", "y")
LINE = ("zh", "zl", "core")
F32 = jnp.float32
BF16 = jnp.bfloat16
I16 = jnp.int16
LIMIT = pltpu.CompilerParams(vmem_limit_bytes=16 << 20)
VMEM = pl.BlockSpec(memory_space=pltpu.VMEM)


def iota(shape, dim):
    return lax.broadcasted_iota(jnp.int32, shape, dim)


def cost(flops, moved):
    return pl.CostEstimate(flops=flops, bytes_accessed=moved, transcendentals=0)


def contract_last(a, b):
    return lax.dot_general(a, b, (((1,), (1,)), ((), ())), preferred_element_type=F32)


def bin_sums(weights, row_of):
    low_ids = iota((BINS // 2, TILE), 0).astype(I16)
    one, zero = BF16(1), BF16(0)
    total = None
    for k in range(ROWS // TILE):
        row = jnp.broadcast_to(row_of(k), (16, TILE))
        low = jnp.concatenate([(row & 127).astype(I16)] * 8, axis=0)
        high = jnp.concatenate([(row >> 7).astype(I16)] * 4, axis=0)
        tile = weights[:, k * TILE : (k + 1) * TILE]
        split = [jnp.where(high == h, tile, zero) for h in range(2)]
        hot = jnp.where(low_ids == low, one, zero)
        piece = contract_last(jnp.concatenate(split, axis=0), hot)
        total = piece if total is None else total + piece
    return total


def stage_kernel(columns, node, margin, labels, feature, cut, weights, pay, chosen):
    here = lax.axis_index("zl") * 2 + lax.axis_index("core")
    feat_start = (
        (lax.axis_index("x") * 8 + lax.axis_index("y")) * 4 + lax.axis_index("zh")
    ) * FEATS
    probability = jax.nn.sigmoid(margin[...])
    gradient = probability - labels[...]
    hessian = probability * (1.0 - probability)
    q = iota((2 * NODES, 1), 0)
    block = q // 16
    block = jnp.where(block < 2, 2 * block + 1, 2 * block - 4)
    node_q = (block * 8 + (q % 16) // 2) ^ (here * 8)
    channel = q % 2
    values = jnp.where(channel == 0, gradient, hessian)
    weights[...] = jnp.where(node[...] == node_q, values, 0.0).astype(BF16)
    local = feature[...] - feat_start
    diagonal = iota((NODES, NODES), 0) == iota((NODES, NODES), 1)
    local_n = jnp.sum(jnp.where(diagonal, local, 0), axis=1, keepdims=True)
    cut_n = jnp.sum(jnp.where(diagonal, cut[...], 0), axis=1, keepdims=True)
    owned_n = (local_n >= 0) & (local_n < FEATS)
    chooser = jnp.where(iota((NODES, FEATS), 1) == local_n, 1.0, 0.0).astype(BF16)
    split_values = jnp.dot(
        chooser, columns[...].astype(F32).astype(BF16), preferred_element_type=F32
    )
    hot = node[...] == iota((NODES, ROWS), 0)
    value = jnp.sum(jnp.where(hot, split_values, 0.0), axis=0, keepdims=True)
    owned = jnp.sum(jnp.where(hot & owned_n, 1.0, 0.0), axis=0, keepdims=True)
    row_cut = jnp.sum(jnp.where(hot, cut_n.astype(F32), 0.0), axis=0, keepdims=True)
    right = jnp.where(value > row_cut, owned, 0.0)
    chosen[...] = jnp.where(owned > 0.5, value, -1.0).astype(jnp.int32)
    sums = bin_sums(weights, lambda k: chosen[:, k * TILE : (k + 1) * TILE])
    sums = jnp.concatenate([sums[:64], sums[64:]], axis=1).astype(BF16).astype(F32)
    cut_q = jnp.sum(
        jnp.where(iota((2 * NODES, NODES), 1) == node_q, cut[...], 0), axis=1, keepdims=True
    )
    below = iota((2 * NODES, BINS), 1) <= cut_q
    left = jnp.sum(jnp.where(below, sums, 0.0), axis=1, keepdims=True)
    whole = jnp.sum(sums, axis=1, keepdims=True)
    lane = iota((2 * NODES, 128), 1)
    slot = 2 * node_q + channel
    entries = jnp.where(lane == slot, left, 0.0) + jnp.where(lane == slot + 64, whole, 0.0)
    half = ROWS // 2
    lines = [
        right[:, i * 128 : (i + 1) * 128] + 2.0 * right[:, half + i * 128 : half + (i + 1) * 128]
        for i in range(8)
    ]
    lines.append(jnp.sum(entries, axis=0, keepdims=True))
    for p in range(32):
        for i in range(9):
            pay[p, i] = lines[i]


def stage(columns, node, margin, labels, feature, cut):
    return pl.pallas_call(
        stage_kernel,
        out_shape=(
            pltpu.VMEM((2 * NODES, ROWS), BF16),
            pltpu.VMEM((32, 9, 1, 128), F32),
        ),
        in_specs=[VMEM] * 6,
        out_specs=[VMEM] * 2,
        scratch_shapes=[pltpu.VMEM((1, ROWS), jnp.int32)],
        name="stage",
        compiler_params=LIMIT,
        cost_estimate=cost(2 * 96 * ROWS * FEATS, 3 << 20),
    )(columns, node, margin, labels, feature, cut)


def histogram_kernel(weights, columns, send, keep):
    def feature(f, carry):
        sums = bin_sums(
            weights, lambda k: columns[pl.ds(f, 1), k * TILE : (k + 1) * TILE]
        ).astype(BF16)
        for h in range(2):
            span = slice(h * 128, (h + 1) * 128)
            send[f, :, span] = sums[64 * h : 64 * h + NODES]
            keep[f, :, span] = sums[64 * h + NODES : 64 * h + 64]
        return carry

    lax.fori_loop(0, FEATS, feature, 0, unroll=8)


def histograms(weights, columns):
    half = pltpu.VMEM((FEATS, NODES, BINS), BF16)
    return pl.pallas_call(
        histogram_kernel,
        out_shape=(half, half),
        in_specs=[VMEM] * 2,
        out_specs=[VMEM] * 2,
        name="histograms",
        compiler_params=LIMIT,
        cost_estimate=cost(2 * 64 * ROWS * FEATS * BINS, 3 << 20),
    )(weights, columns)


def chip_sum_kernel(keep, arrived, own, send):
    for f in range(0, FEATS, 8):
        total = keep[f : f + 8].astype(F32) + arrived[f : f + 8].astype(F32)
        own[f : f + 8] = total[:, :16]
        send[f : f + 8] = total[:, 16:].astype(BF16)


def chip_sum(keep, arrived):
    return pl.pallas_call(
        chip_sum_kernel,
        out_shape=(
            pltpu.VMEM((FEATS, 16, BINS), F32),
            pltpu.VMEM((FEATS, 16, BINS), BF16),
        ),
        in_specs=[VMEM] * 2,
        out_specs=[VMEM] * 2,
        name="chip_sum",
        compiler_params=LIMIT,
        cost_estimate=cost(FEATS * 32 * BINS, 3 << 20),
    )(keep, arrived)


def relay_kernel(plane, pay):
    for i in range(9):
        line = plane[0, i]
        for p in range(1, 32):
            line = line + plane[p, i]
        for p in range(16):
            pay[p, i] = line


def relay(plane):
    return pl.pallas_call(
        relay_kernel,
        out_shape=pltpu.VMEM((16, 9, 1, 128), F32),
        in_specs=[VMEM],
        out_specs=VMEM,
        name="relay",
        compiler_params=LIMIT,
        cost_estimate=cost(32 * 9 * 128, 1 << 17),
    )(plane)


def finish_kernel(own, arrived, histogram, total):
    for f in range(0, FEATS, 8):
        piece = (own[f : f + 8] + arrived[f : f + 8].astype(F32)).reshape(128, BINS)
        for h in range(2):
            total[h, f * 16 : (f + 8) * 16, :] = piece[:, h * 128 : (h + 1) * 128]
    for q in range(16):
        for h in range(2):
            histogram[q, :, h * 128 : (h + 1) * 128] = total[h, pl.ds(q, FEATS, stride=16), :]


def finish(own, arrived):
    return pl.pallas_call(
        finish_kernel,
        out_shape=jax.ShapeDtypeStruct((16, FEATS, BINS), F32),
        in_specs=[VMEM] * 2,
        out_specs=VMEM,
        scratch_shapes=[pltpu.VMEM((2, FEATS * 16, 128), F32)],
        name="finish",
        compiler_params=LIMIT,
        cost_estimate=cost(FEATS * 16 * BINS, 3 << 20),
    )(own, arrived)


def rows_kernel(parts, node, margin, labels, margin_out, child_out, grad_out, codes_ref):
    here = lax.axis_index("zl") * 2 + lax.axis_index("core")
    for i in range(8):
        line = parts[here, i]
        for z in range(1, 4):
            line = line + parts[4 * z + here, i]
        codes_ref[i : i + 1, :] = line
    table = parts[0, 8]
    for m in range(1, 16):
        table = table + parts[m, 8]
    codes = codes_ref[...]
    table = jnp.broadcast_to(table, (8, 128))
    rest = pltpu.roll(table, 64, 1) - table
    leaf_left = -table / (pltpu.roll(table, 127, 1) + 1.0)
    leaf_right = -rest / (pltpu.roll(rest, 127, 1) + 1.0)
    high = jnp.where(codes > 1.5, 1.0, 0.0)
    go_right = jnp.concatenate([codes - 2.0 * high, high], axis=0) > 0.5
    node_here = node[...]
    shift = jnp.zeros((16, 128), F32)
    for n in range(NODES):
        step = jnp.where(
            go_right,
            jnp.broadcast_to(leaf_right[0:1, 2 * n : 2 * n + 1], (16, 128)),
            jnp.broadcast_to(leaf_left[0:1, 2 * n : 2 * n + 1], (16, 128)),
        )
        shift = jnp.where(node_here == n, step, shift)
    moved = margin[...] + shift
    margin_out[...] = moved
    child_out[...] = 2 * node_here + jnp.where(go_right, 1, 0)
    fresh = jax.nn.sigmoid(moved)
    slope = fresh - labels[...]
    curve = fresh * (1.0 - fresh)
    for i in range(16):
        grad_out[0:1, i * 128 : (i + 1) * 128] = slope[i : i + 1, :]
        grad_out[1:2, i * 128 : (i + 1) * 128] = curve[i : i + 1, :]


def rows_update(parts, node, margin, labels):
    return pl.pallas_call(
        rows_kernel,
        out_shape=(
            jax.ShapeDtypeStruct((16, 128), F32),
            jax.ShapeDtypeStruct((16, 128), jnp.int32),
            jax.ShapeDtypeStruct((2, ROWS), F32),
        ),
        in_specs=[VMEM] * 4,
        out_specs=[VMEM] * 3,
        scratch_shapes=[pltpu.VMEM((8, 128), F32)],
        name="rows_update",
        compiler_params=LIMIT,
        cost_estimate=cost(ROWS * 128, 1 << 17),
    )(parts, node, margin, labels)


def share(spread, axes):
    return lax.all_to_all(spread, axes, 0, 0, tiled=True)


def near(array):
    return pltpu.with_memory_space_constraint(array, pltpu.VMEM)


def far(array):
    return pltpu.with_memory_space_constraint(array, pltpu.HBM)


def on_device(binned, node_of, margin, labels, split_feature, split_bin):
    swap = [(0, 1), (1, 0)]
    columns = binned.T
    weights, pay = stage(
        far(columns),
        far(node_of.reshape(1, ROWS)),
        far(margin.reshape(1, ROWS)),
        far(labels.reshape(1, ROWS)),
        far(split_feature.reshape(1, NODES)),
        far(split_bin.reshape(1, NODES)),
    )
    plane = share(pay, PLANE)
    send, keep = histograms(near(weights), columns)
    arrived = lax.ppermute(send, "core", swap)
    pay = relay(near(plane))
    own, send_line = chip_sum(near(keep), near(arrived))
    arrived = lax.ppermute(send_line, "zl", swap)
    parts = share(pay, LINE)
    histogram = finish(near(own), near(arrived))
    margin_out, child_out, grad_out = rows_update(
        near(parts),
        near(node_of.reshape(16, 128)),
        near(margin.reshape(16, 128)),
        near(labels.reshape(16, 128)),
    )
    return (
        histogram.reshape(8, 2, FEATS, BINS),
        margin_out.reshape(ROWS),
        child_out.reshape(ROWS),
        grad_out,
    )


def solution(mesh):
    fine = Mesh(mesh.devices.reshape(4, 8, 4, 2, 2), ("x", "y", "zh", "zl", "core"))
    rows = P(ROW_AXES)
    in_specs = (P(ROW_AXES, FEAT_AXES), rows, rows, rows, P(), P())
    out_specs = (P(ROW_AXES, None, FEAT_AXES, None), rows, rows, P(None, ROW_AXES))

    return jax.shard_map(
        on_device, mesh=fine, in_specs=in_specs, out_specs=out_specs, check_vma=False
    )
```

```python
import jax
import jax.numpy as jnp
from jax import lax
from jax.experimental import pallas as pl
from jax.experimental.pallas import tpu as pltpu
from jax.sharding import Mesh
from jax.sharding import PartitionSpec as P

BINS = 256
NODES = 32
ROWS = 2048
FEATS = 64
TILE = 256
FEAT_AXES = ("x", "y", "zh")
ROW_AXES = ("zl", "core")
PLANE = ("x", "y")
LINE = ("zh", "zl", "core")
F32 = jnp.float32
BF16 = jnp.bfloat16
I16 = jnp.int16
LIMIT = pltpu.CompilerParams(vmem_limit_bytes=16 << 20)
VMEM = pl.BlockSpec(memory_space=pltpu.VMEM)


def iota(shape, dim):
    return lax.broadcasted_iota(jnp.int32, shape, dim)


def cost(flops, moved):
    return pl.CostEstimate(flops=flops, bytes_accessed=moved, transcendentals=0)


def contract_last(a, b):
    return lax.dot_general(a, b, (((1,), (1,)), ((), ())), preferred_element_type=F32)


def bin_sums(weights, row_of):
    low_ids = iota((BINS // 2, TILE), 0).astype(I16)
    one, zero = BF16(1), BF16(0)
    total = None
    for k in range(ROWS // TILE):
        row = jnp.broadcast_to(row_of(k), (16, TILE))
        low = jnp.concatenate([(row & 127).astype(I16)] * 8, axis=0)
        high = jnp.concatenate([(row >> 7).astype(I16)] * 4, axis=0)
        tile = weights[:, k * TILE : (k + 1) * TILE]
        split = [jnp.where(high == h, tile, zero) for h in range(2)]
        hot = jnp.where(low_ids == low, one, zero)
        piece = contract_last(jnp.concatenate(split, axis=0), hot)
        total = piece if total is None else total + piece
    return total


def stage_kernel(columns, node, margin, labels, feature, cut, weights, pay, chosen):
    here = lax.axis_index("zl") * 2 + lax.axis_index("core")
    feat_start = (
        (lax.axis_index("x") * 8 + lax.axis_index("y")) * 4 + lax.axis_index("zh")
    ) * FEATS
    probability = jax.nn.sigmoid(margin[...])
    gradient = probability - labels[...]
    hessian = probability * (1.0 - probability)
    q = iota((2 * NODES, 1), 0)
    block = q // 16
    block = jnp.where(block < 2, 2 * block + 1, 2 * block - 4)
    node_q = (block * 8 + (q % 16) // 2) ^ (here * 8)
    channel = q % 2
    values = jnp.where(channel == 0, gradient, hessian)
    weights[...] = jnp.where(node[...] == node_q, values, 0.0).astype(BF16)
    local = feature[...] - feat_start
    diagonal = iota((NODES, NODES), 0) == iota((NODES, NODES), 1)
    local_n = jnp.sum(jnp.where(diagonal, local, 0), axis=1, keepdims=True)
    cut_n = jnp.sum(jnp.where(diagonal, cut[...], 0), axis=1, keepdims=True)
    owned_n = (local_n >= 0) & (local_n < FEATS)
    chooser = jnp.where(iota((NODES, FEATS), 1) == local_n, 1.0, 0.0).astype(BF16)
    split_values = jnp.dot(
        chooser, columns[...].astype(F32).astype(BF16), preferred_element_type=F32
    )
    hot = node[...] == iota((NODES, ROWS), 0)
    value = jnp.sum(jnp.where(hot, split_values, 0.0), axis=0, keepdims=True)
    owned = jnp.sum(jnp.where(hot & owned_n, 1.0, 0.0), axis=0, keepdims=True)
    row_cut = jnp.sum(jnp.where(hot, cut_n.astype(F32), 0.0), axis=0, keepdims=True)
    right = jnp.where(value > row_cut, owned, 0.0)
    chosen[...] = jnp.where(owned > 0.5, value, -1.0).astype(jnp.int32)
    sums = bin_sums(weights, lambda k: chosen[:, k * TILE : (k + 1) * TILE])
    sums = jnp.concatenate([sums[:64], sums[64:]], axis=1).astype(BF16).astype(F32)
    cut_q = jnp.sum(
        jnp.where(iota((2 * NODES, NODES), 1) == node_q, cut[...], 0), axis=1, keepdims=True
    )
    below = iota((2 * NODES, BINS), 1) <= cut_q
    left = jnp.sum(jnp.where(below, sums, 0.0), axis=1, keepdims=True)
    whole = jnp.sum(sums, axis=1, keepdims=True)
    lane = iota((2 * NODES, 128), 1)
    slot = 2 * node_q + channel
    entries = jnp.where(lane == slot, left, 0.0) + jnp.where(lane == slot + 64, whole, 0.0)
    half = ROWS // 2
    lines = [
        right[:, i * 128 : (i + 1) * 128] + 2.0 * right[:, half + i * 128 : half + (i + 1) * 128]
        for i in range(8)
    ]
    lines.append(jnp.sum(entries, axis=0, keepdims=True))
    for p in range(16):
        for i in range(9):
            pay[p, i] = lines[i]


def stage(columns, node, margin, labels, feature, cut):
    return pl.pallas_call(
        stage_kernel,
        out_shape=(
            pltpu.VMEM((2 * NODES, ROWS), BF16),
            pltpu.VMEM((16, 9, 1, 128), F32),
        ),
        in_specs=[VMEM] * 6,
        out_specs=[VMEM] * 2,
        scratch_shapes=[pltpu.VMEM((1, ROWS), jnp.int32)],
        name="stage",
        compiler_params=LIMIT,
        cost_estimate=cost(2 * 96 * ROWS * FEATS, 3 << 20),
    )(columns, node, margin, labels, feature, cut)


def histogram_kernel(weights, columns, send, keep):
    def feature(f, carry):
        sums = bin_sums(
            weights, lambda k: columns[pl.ds(f, 1), k * TILE : (k + 1) * TILE]
        ).astype(BF16)
        for h in range(2):
            span = slice(h * 128, (h + 1) * 128)
            send[f, :, span] = sums[64 * h : 64 * h + NODES]
            keep[f, :, span] = sums[64 * h + NODES : 64 * h + 64]
        return carry

    lax.fori_loop(0, FEATS, feature, 0, unroll=8)


def histograms(weights, columns):
    half = pltpu.VMEM((FEATS, NODES, BINS), BF16)
    return pl.pallas_call(
        histogram_kernel,
        out_shape=(half, half),
        in_specs=[VMEM] * 2,
        out_specs=[VMEM] * 2,
        name="histograms",
        compiler_params=LIMIT,
        cost_estimate=cost(2 * 64 * ROWS * FEATS * BINS, 3 << 20),
    )(weights, columns)


def chip_sum_kernel(keep, arrived, own, send):
    for f in range(0, FEATS, 8):
        total = keep[f : f + 8].astype(F32) + arrived[f : f + 8].astype(F32)
        own[f : f + 8] = total[:, :16]
        send[f : f + 8] = total[:, 16:].astype(BF16)


def chip_sum(keep, arrived):
    return pl.pallas_call(
        chip_sum_kernel,
        out_shape=(
            pltpu.VMEM((FEATS, 16, BINS), F32),
            pltpu.VMEM((FEATS, 16, BINS), BF16),
        ),
        in_specs=[VMEM] * 2,
        out_specs=[VMEM] * 2,
        name="chip_sum",
        compiler_params=LIMIT,
        cost_estimate=cost(FEATS * 32 * BINS, 3 << 20),
    )(keep, arrived)


def relay_kernel(line, pay):
    here = lax.axis_index("zl") * 2 + lax.axis_index("core")
    for i in range(9):
        total = line[here, i] if i < 8 else line[0, i]
        for m in range(1, 4 if i < 8 else 16):
            total = total + (line[4 * m + here, i] if i < 8 else line[m, i])
        for p in range(32):
            pay[p, i] = total


def relay(line):
    return pl.pallas_call(
        relay_kernel,
        out_shape=pltpu.VMEM((32, 9, 1, 128), F32),
        in_specs=[VMEM],
        out_specs=VMEM,
        name="relay",
        compiler_params=LIMIT,
        cost_estimate=cost(32 * 9 * 128, 1 << 17),
    )(line)


def finish_kernel(own, arrived, histogram, total):
    for f in range(0, FEATS, 8):
        piece = (own[f : f + 8] + arrived[f : f + 8].astype(F32)).reshape(128, BINS)
        for h in range(2):
            total[h, f * 16 : (f + 8) * 16, :] = piece[:, h * 128 : (h + 1) * 128]
    for q in range(16):
        for h in range(2):
            histogram[q, :, h * 128 : (h + 1) * 128] = total[h, pl.ds(q, FEATS, stride=16), :]


def finish(own, arrived):
    return pl.pallas_call(
        finish_kernel,
        out_shape=jax.ShapeDtypeStruct((16, FEATS, BINS), F32),
        in_specs=[VMEM] * 2,
        out_specs=VMEM,
        scratch_shapes=[pltpu.VMEM((2, FEATS * 16, 128), F32)],
        name="finish",
        compiler_params=LIMIT,
        cost_estimate=cost(FEATS * 16 * BINS, 3 << 20),
    )(own, arrived)


def rows_kernel(parts, node, margin, labels, margin_out, child_out, grad_out, codes_ref):
    for i in range(8):
        line = parts[0, i]
        for p in range(1, 32):
            line = line + parts[p, i]
        codes_ref[i : i + 1, :] = line
    table = parts[0, 8]
    for p in range(1, 32):
        table = table + parts[p, 8]
    codes = codes_ref[...]
    table = jnp.broadcast_to(table, (8, 128))
    rest = pltpu.roll(table, 64, 1) - table
    leaf_left = -table / (pltpu.roll(table, 127, 1) + 1.0)
    leaf_right = -rest / (pltpu.roll(rest, 127, 1) + 1.0)
    high = jnp.where(codes > 1.5, 1.0, 0.0)
    go_right = jnp.concatenate([codes - 2.0 * high, high], axis=0) > 0.5
    node_here = node[...]
    shift = jnp.zeros((16, 128), F32)
    for n in range(NODES):
        step = jnp.where(
            go_right,
            jnp.broadcast_to(leaf_right[0:1, 2 * n : 2 * n + 1], (16, 128)),
            jnp.broadcast_to(leaf_left[0:1, 2 * n : 2 * n + 1], (16, 128)),
        )
        shift = jnp.where(node_here == n, step, shift)
    moved = margin[...] + shift
    margin_out[...] = moved
    child_out[...] = 2 * node_here + jnp.where(go_right, 1, 0)
    fresh = jax.nn.sigmoid(moved)
    slope = fresh - labels[...]
    curve = fresh * (1.0 - fresh)
    for i in range(16):
        grad_out[0:1, i * 128 : (i + 1) * 128] = slope[i : i + 1, :]
        grad_out[1:2, i * 128 : (i + 1) * 128] = curve[i : i + 1, :]


def rows_update(parts, node, margin, labels):
    return pl.pallas_call(
        rows_kernel,
        out_shape=(
            jax.ShapeDtypeStruct((16, 128), F32),
            jax.ShapeDtypeStruct((16, 128), jnp.int32),
            jax.ShapeDtypeStruct((2, ROWS), F32),
        ),
        in_specs=[VMEM] * 4,
        out_specs=[VMEM] * 3,
        scratch_shapes=[pltpu.VMEM((8, 128), F32)],
        name="rows_update",
        compiler_params=LIMIT,
        cost_estimate=cost(ROWS * 128, 1 << 17),
    )(parts, node, margin, labels)


def share(spread, axes):
    return lax.all_to_all(spread, axes, 0, 0, tiled=True)


def near(array):
    return pltpu.with_memory_space_constraint(array, pltpu.VMEM)


def far(array):
    return pltpu.with_memory_space_constraint(array, pltpu.HBM)


def on_device(binned, node_of, margin, labels, split_feature, split_bin):
    swap = [(0, 1), (1, 0)]
    columns = binned.T
    weights, pay = stage(
        far(columns),
        far(node_of.reshape(1, ROWS)),
        far(margin.reshape(1, ROWS)),
        far(labels.reshape(1, ROWS)),
        far(split_feature.reshape(1, NODES)),
        far(split_bin.reshape(1, NODES)),
    )
    line = share(pay, LINE)
    send, keep = histograms(near(weights), columns)
    arrived = lax.ppermute(near(send), "core", swap)
    pay = relay(near(line))
    own, send_line = chip_sum(near(keep), near(arrived))
    arrived = lax.ppermute(near(send_line), "zl", swap)
    parts = share(pay, PLANE)
    histogram = finish(near(own), near(arrived))
    margin_out, child_out, grad_out = rows_update(
        near(parts),
        near(node_of.reshape(16, 128)),
        near(margin.reshape(16, 128)),
        near(labels.reshape(16, 128)),
    )
    return (
        histogram.reshape(8, 2, FEATS, BINS),
        margin_out.reshape(ROWS),
        child_out.reshape(ROWS),
        grad_out,
    )


def solution(mesh):
    fine = Mesh(mesh.devices.reshape(4, 8, 4, 2, 2), ("x", "y", "zh", "zl", "core"))
    rows = P(ROW_AXES)
    in_specs = (P(ROW_AXES, FEAT_AXES), rows, rows, rows, P(), P())
    out_specs = (P(ROW_AXES, None, FEAT_AXES, None), rows, rows, P(None, ROW_AXES))

    return jax.shard_map(
        on_device, mesh=fine, in_specs=in_specs, out_specs=out_specs, check_vma=False
    )
```

```python
import functools

import jax
import jax.numpy as jnp
from jax import lax
from jax.experimental import pallas as pl
from jax.experimental.pallas import tpu as pltpu
from jax.sharding import Mesh
from jax.sharding import PartitionSpec as P

BINS = 256
NODES = 32
ROWS = 2048
FEATS = 64
TILE = 256
CUT = 48
FEAT_AXES = ("x", "y", "zh")
ROW_AXES = ("zl", "core")
PLANE = ("x", "y")
LINE = ("zh", "zl", "core")
F32 = jnp.float32
BF16 = jnp.bfloat16
I16 = jnp.int16
LIMIT = pltpu.CompilerParams(vmem_limit_bytes=16 << 20)
VMEM = pl.BlockSpec(memory_space=pltpu.VMEM)


def near(array):
    return pltpu.with_memory_space_constraint(array, pltpu.VMEM)


def far(array):
    return pltpu.with_memory_space_constraint(array, pltpu.HBM)


def iota(shape, dim):
    return lax.broadcasted_iota(jnp.int32, shape, dim)


def cost(flops, moved):
    return pl.CostEstimate(flops=flops, bytes_accessed=moved, transcendentals=0)


def contract_last(a, b):
    return lax.dot_general(a, b, (((1,), (1,)), ((), ())), preferred_element_type=F32)


def bin_sums(weights, row_of):
    low_ids = iota((BINS // 2, TILE), 0).astype(I16)
    one, zero = BF16(1), BF16(0)
    total = None
    for k in range(ROWS // TILE):
        row = jnp.broadcast_to(row_of(k), (16, TILE))
        low = jnp.concatenate([(row & 127).astype(I16)] * 8, axis=0)
        high = jnp.concatenate([(row >> 7).astype(I16)] * 4, axis=0)
        tile = weights[:, k * TILE : (k + 1) * TILE]
        split = [jnp.where(high == h, tile, zero) for h in range(2)]
        hot = jnp.where(low_ids == low, one, zero)
        piece = contract_last(jnp.concatenate(split, axis=0), hot)
        total = piece if total is None else total + piece
    return total


def pair_sums(weights, row_of, row_of_next):
    low_ids = iota((BINS // 2, TILE), 0).astype(I16)
    one, zero = BF16(1), BF16(0)
    total = None
    for k in range(ROWS // TILE):
        tile = weights[:, k * TILE : (k + 1) * TILE]
        parts, hots = [tile], []
        for source in (row_of, row_of_next):
            row = jnp.broadcast_to(source(k), (16, TILE))
            low = jnp.concatenate([(row & 127).astype(I16)] * 8, axis=0)
            high = jnp.concatenate([(row >> 7).astype(I16)] * 4, axis=0)
            parts.append(jnp.where(high == 1, tile, zero))
            hots.append(jnp.where(low_ids == low, one, zero))
        piece = contract_last(jnp.concatenate(parts, axis=0), jnp.concatenate(hots, axis=0))
        total = piece if total is None else total + piece
    sums = []
    for i in range(2):
        span = slice(i * 128, (i + 1) * 128)
        upper = total[64 * (i + 1) : 64 * (i + 2), span]
        sums.append((total[:64, span] - upper, upper))
    return sums


def stage_kernel(columns, node, margin, labels, feature, cut, weights, pay, chosen):
    here = lax.axis_index("zl") * 2 + lax.axis_index("core")
    feat_start = (
        (lax.axis_index("x") * 8 + lax.axis_index("y")) * 4 + lax.axis_index("zh")
    ) * FEATS
    probability = jax.nn.sigmoid(margin[...])
    gradient = probability - labels[...]
    hessian = probability * (1.0 - probability)
    q = iota((2 * NODES, 1), 0)
    block = q // 16
    block = jnp.where(block < 2, 2 * block + 1, 2 * block - 4)
    node_q = (block * 8 + (q % 16) // 2) ^ (here * 8)
    channel = q % 2
    values = jnp.where(channel == 0, gradient, hessian)
    weights[...] = jnp.where(node[...] == node_q, values, 0.0).astype(BF16)
    local = feature[...] - feat_start
    diagonal = iota((NODES, NODES), 0) == iota((NODES, NODES), 1)
    local_n = jnp.sum(jnp.where(diagonal, local, 0), axis=1, keepdims=True)
    cut_n = jnp.sum(jnp.where(diagonal, cut[...], 0), axis=1, keepdims=True)
    owned_n = (local_n >= 0) & (local_n < FEATS)
    chooser = jnp.where(iota((NODES, FEATS), 1) == local_n, 1.0, 0.0).astype(BF16)
    split_values = jnp.dot(
        chooser, columns[...].astype(F32).astype(BF16), preferred_element_type=F32
    )
    hot = node[...] == iota((NODES, ROWS), 0)
    value = jnp.sum(jnp.where(hot, split_values, 0.0), axis=0, keepdims=True)
    owned = jnp.sum(jnp.where(hot & owned_n, 1.0, 0.0), axis=0, keepdims=True)
    row_cut = jnp.sum(jnp.where(hot, cut_n.astype(F32), 0.0), axis=0, keepdims=True)
    right = jnp.where(value > row_cut, owned, 0.0)
    chosen[...] = jnp.where(owned > 0.5, value, -1.0).astype(jnp.int32)
    sums = bin_sums(weights, lambda k: chosen[:, k * TILE : (k + 1) * TILE])
    sums = jnp.concatenate([sums[:64], sums[64:]], axis=1).astype(BF16).astype(F32)
    cut_q = jnp.sum(
        jnp.where(iota((2 * NODES, NODES), 1) == node_q, cut[...], 0), axis=1, keepdims=True
    )
    below = iota((2 * NODES, BINS), 1) <= cut_q
    left = jnp.sum(jnp.where(below, sums, 0.0), axis=1, keepdims=True)
    whole = jnp.sum(sums, axis=1, keepdims=True)
    lane = iota((2 * NODES, 128), 1)
    slot = 2 * node_q + channel
    entries = jnp.where(lane == slot, left, 0.0) + jnp.where(lane == slot + 64, whole, 0.0)
    half = ROWS // 2
    lines = [
        right[:, i * 128 : (i + 1) * 128] + 2.0 * right[:, half + i * 128 : half + (i + 1) * 128]
        for i in range(8)
    ]
    lines.append(jnp.sum(entries, axis=0, keepdims=True))
    for p in range(16):
        for i in range(9):
            pay[p, i] = lines[i]


def stage(columns, node, margin, labels, feature, cut):
    return pl.pallas_call(
        stage_kernel,
        out_shape=(
            pltpu.VMEM((2 * NODES, ROWS), BF16),
            pltpu.VMEM((16, 9, 1, 128), F32),
        ),
        in_specs=[VMEM] * 6,
        out_specs=[VMEM] * 2,
        scratch_shapes=[pltpu.VMEM((1, ROWS), jnp.int32)],
        name="stage",
        compiler_params=LIMIT,
        cost_estimate=cost(2 * 96 * ROWS * FEATS, 3 << 20),
    )(columns, node, margin, labels, feature, cut)


def histogram_kernel(first, count, weights, columns, send, keep):
    def pair(p, carry):
        f = 2 * p

        def source(g):
            return lambda k: columns[pl.ds(first + g, 1), k * TILE : (k + 1) * TILE]

        for i, halves in enumerate(pair_sums(weights, source(f), source(f + 1))):
            for h in range(2):
                span = slice(h * 128, (h + 1) * 128)
                sums = halves[h].astype(BF16)
                send[f + i, :, span] = sums[:NODES]
                keep[f + i, :, span] = sums[NODES:]
        return carry

    lax.fori_loop(0, count // 2, pair, 0, unroll=4)


def histograms(weights, columns, first, count):
    half = pltpu.VMEM((count, NODES, BINS), BF16)
    return pl.pallas_call(
        functools.partial(histogram_kernel, first, count),
        out_shape=(half, half),
        in_specs=[VMEM] * 2,
        out_specs=[VMEM] * 2,
        compiler_params=LIMIT,
        cost_estimate=cost(2 * 64 * ROWS * count * BINS, 3 << 20),
    )(weights, columns)


def chip_sum_kernel(keep, arrived, sent, own, send):
    for f in range(0, keep.shape[0], 8):
        total = keep[f : f + 8].astype(F32) + arrived[f : f + 8].astype(F32)
        own[f : f + 8] = total[:, :16]
        send[f : f + 8] = total[:, 16:].astype(BF16)


def chip_sum(keep, arrived, sent):
    count = keep.shape[0]
    return pl.pallas_call(
        chip_sum_kernel,
        out_shape=(
            pltpu.VMEM((count, 16, BINS), F32),
            pltpu.VMEM((count, 16, BINS), BF16),
        ),
        in_specs=[VMEM, VMEM, pl.BlockSpec(memory_space=pl.ANY)],
        out_specs=[VMEM] * 2,
        name="chip_sum",
        compiler_params=LIMIT,
        cost_estimate=cost(count * 32 * BINS, 3 << 20),
    )(near(keep), near(arrived), near(sent))


def relay_kernel(line, sent, pay):
    here = lax.axis_index("zl") * 2 + lax.axis_index("core")
    for i in range(9):
        total = line[here, i] if i < 8 else line[0, i]
        for m in range(1, 4 if i < 8 else 16):
            total = total + (line[4 * m + here, i] if i < 8 else line[m, i])
        for p in range(32):
            pay[p, i] = total


def relay(line, sent):
    return pl.pallas_call(
        relay_kernel,
        out_shape=pltpu.VMEM((32, 9, 1, 128), F32),
        in_specs=[VMEM, pl.BlockSpec(memory_space=pl.ANY)],
        out_specs=VMEM,
        name="relay",
        compiler_params=LIMIT,
        cost_estimate=cost(32 * 9 * 128, 1 << 17),
    )(near(line), near(sent))


def finish_kernel(count, own, arrived, sent, *rest):
    histogram, total = rest[-2:]
    for f in range(0, count, 8):
        piece = (own[f : f + 8] + arrived[f : f + 8].astype(F32)).reshape(128, BINS)
        for h in range(2):
            total[h, f * 16 : (f + 8) * 16, :] = piece[:, h * 128 : (h + 1) * 128]
    for q in range(16):
        for h in range(2):
            histogram[q, :, h * 128 : (h + 1) * 128] = total[h, pl.ds(q, count, stride=16), :]


def finish(own, arrived, sent, first, so_far=None):
    count = own.shape[0]
    anywhere = pl.BlockSpec(memory_space=pl.ANY)
    more = () if so_far is None else (so_far,)
    return pl.pallas_call(
        functools.partial(finish_kernel, count),
        out_shape=jax.ShapeDtypeStruct((16, FEATS, BINS), F32),
        grid=(1,),
        in_specs=[VMEM, VMEM, anywhere] + [anywhere] * len(more),
        out_specs=pl.BlockSpec((16, count, BINS), lambda i: (0, first // count, 0)),
        scratch_shapes=[pltpu.VMEM((2, count * 16, 128), F32)],
        input_output_aliases={3: 0} if more else {},
        compiler_params=LIMIT,
        cost_estimate=cost(count * 16 * BINS, 3 << 20),
    )(near(own), near(arrived), near(sent), *more)


def rows_kernel(parts, node, margin, labels, sent, margin_out, child_out, grad_out, codes_ref):
    for i in range(8):
        line = parts[0, i]
        for p in range(1, 32):
            line = line + parts[p, i]
        codes_ref[i : i + 1, :] = line
    table = parts[0, 8]
    for p in range(1, 32):
        table = table + parts[p, 8]
    codes = codes_ref[...]
    table = jnp.broadcast_to(table, (8, 128))
    rest = pltpu.roll(table, 64, 1) - table
    leaf_left = -table / (pltpu.roll(table, 127, 1) + 1.0)
    leaf_right = -rest / (pltpu.roll(rest, 127, 1) + 1.0)
    high = jnp.where(codes > 1.5, 1.0, 0.0)
    go_right = jnp.concatenate([codes - 2.0 * high, high], axis=0) > 0.5
    node_here = node[...]
    shift = jnp.zeros((16, 128), F32)
    for n in range(NODES):
        step = jnp.where(
            go_right,
            jnp.broadcast_to(leaf_right[0:1, 2 * n : 2 * n + 1], (16, 128)),
            jnp.broadcast_to(leaf_left[0:1, 2 * n : 2 * n + 1], (16, 128)),
        )
        shift = jnp.where(node_here == n, step, shift)
    moved = margin[...] + shift
    margin_out[...] = moved
    child_out[...] = 2 * node_here + jnp.where(go_right, 1, 0)
    fresh = jax.nn.sigmoid(moved)
    slope = fresh - labels[...]
    curve = fresh * (1.0 - fresh)
    for i in range(16):
        grad_out[0:1, i * 128 : (i + 1) * 128] = slope[i : i + 1, :]
        grad_out[1:2, i * 128 : (i + 1) * 128] = curve[i : i + 1, :]


def rows_update(parts, node, margin, labels, sent):
    return pl.pallas_call(
        rows_kernel,
        out_shape=(
            jax.ShapeDtypeStruct((16, 128), F32),
            jax.ShapeDtypeStruct((16, 128), jnp.int32),
            jax.ShapeDtypeStruct((2, ROWS), F32),
        ),
        in_specs=[VMEM] * 4 + [pl.BlockSpec(memory_space=pl.ANY)],
        out_specs=[VMEM] * 3,
        scratch_shapes=[pltpu.VMEM((8, 128), F32)],
        name="rows_update",
        compiler_params=LIMIT,
        cost_estimate=cost(ROWS * 128, 1 << 17),
    )(parts, node, margin, labels, near(sent))


def share(spread, axes):
    return lax.all_to_all(spread, axes, 0, 0, tiled=True)


def on_device(binned, node_of, margin, labels, split_feature, split_bin):
    swap = [(0, 1), (1, 0)]
    columns = binned.T
    weights, pay = stage(
        far(columns),
        far(node_of.reshape(1, ROWS)),
        far(margin.reshape(1, ROWS)),
        far(labels.reshape(1, ROWS)),
        far(split_feature.reshape(1, NODES)),
        far(split_bin.reshape(1, NODES)),
    )
    line = share(pay, LINE)
    send_a, keep_a = histograms(near(weights), near(columns), 0, CUT)
    arrived_a = lax.ppermute(send_a, "core", swap)
    pay = relay(line, pay)
    parts = share(pay, PLANE)
    own_a, line_a = chip_sum(keep_a, arrived_a, send_a)
    arrived_a = lax.ppermute(line_a, "zl", swap)
    send_b, keep_b = histograms(near(weights), near(columns), CUT, FEATS - CUT)
    arrived_b = lax.ppermute(send_b, "core", swap)
    own_b, line_b = chip_sum(keep_b, arrived_b, send_b)
    arrived_b = lax.ppermute(line_b, "zl", swap)
    histogram = finish(own_a, arrived_a, line_a, 0)
    margin_out, child_out, grad_out = rows_update(
        near(parts),
        near(node_of.reshape(16, 128)),
        near(margin.reshape(16, 128)),
        near(labels.reshape(16, 128)),
        pay,
    )
    histogram = finish(own_b, arrived_b, line_b, CUT, histogram)
    return (
        histogram.reshape(8, 2, FEATS, BINS),
        margin_out.reshape(ROWS),
        child_out.reshape(ROWS),
        grad_out,
    )


def solution(mesh):
    fine = Mesh(mesh.devices.reshape(4, 8, 4, 2, 2), ("x", "y", "zh", "zl", "core"))
    rows = P(ROW_AXES)
    in_specs = (P(ROW_AXES, FEAT_AXES), rows, rows, rows, P(), P())
    out_specs = (P(ROW_AXES, None, FEAT_AXES, None), rows, rows, P(None, ROW_AXES))

    return jax.shard_map(
        on_device, mesh=fine, in_specs=in_specs, out_specs=out_specs, check_vma=False
    )
```

```python
import functools

import jax
import jax.numpy as jnp
from jax import lax
from jax.experimental import pallas as pl
from jax.experimental.pallas import tpu as pltpu
from jax.sharding import Mesh
from jax.sharding import PartitionSpec as P

BINS = 256
NODES = 32
ROWS = 2048
FEATS = 64
TILE = 256
CUT = 48
FEAT_AXES = ("x", "y", "zh")
ROW_AXES = ("zl", "core")
PLANE = ("x", "y")
LINE = ("zh", "zl", "core")
F32 = jnp.float32
BF16 = jnp.bfloat16
I16 = jnp.int16
LIMIT = pltpu.CompilerParams(vmem_limit_bytes=16 << 20)
VMEM = pl.BlockSpec(memory_space=pltpu.VMEM)


def near(array):
    return pltpu.with_memory_space_constraint(array, pltpu.VMEM)


def far(array):
    return pltpu.with_memory_space_constraint(array, pltpu.HBM)


def iota(shape, dim):
    return lax.broadcasted_iota(jnp.int32, shape, dim)


def cost(flops, moved):
    return pl.CostEstimate(flops=flops, bytes_accessed=moved, transcendentals=0)


def contract_last(a, b):
    return lax.dot_general(a, b, (((1,), (1,)), ((), ())), preferred_element_type=F32)


def bin_sums(weights, row_of):
    low_ids = iota((BINS // 2, TILE), 0).astype(I16)
    one, zero = BF16(1), BF16(0)
    total = None
    for k in range(ROWS // TILE):
        row = jnp.broadcast_to(row_of(k), (16, TILE))
        low = jnp.concatenate([(row & 127).astype(I16)] * 8, axis=0)
        high = jnp.concatenate([(row >> 7).astype(I16)] * 4, axis=0)
        tile = weights[:, k * TILE : (k + 1) * TILE]
        split = [jnp.where(high == h, tile, zero) for h in range(2)]
        hot = jnp.where(low_ids == low, one, zero)
        piece = contract_last(jnp.concatenate(split, axis=0), hot)
        total = piece if total is None else total + piece
    return total


def stage_kernel(columns, node, margin, labels, feature, cut, weights, pay, chosen):
    here = lax.axis_index("zl") * 2 + lax.axis_index("core")
    feat_start = (
        (lax.axis_index("x") * 8 + lax.axis_index("y")) * 4 + lax.axis_index("zh")
    ) * FEATS
    probability = jax.nn.sigmoid(margin[...])
    gradient = probability - labels[...]
    hessian = probability * (1.0 - probability)
    q = iota((2 * NODES, 1), 0)
    block = q // 16
    block = jnp.where(block < 2, 2 * block + 1, 2 * block - 4)
    node_q = (block * 8 + (q % 16) // 2) ^ (here * 8)
    channel = q % 2
    values = jnp.where(channel == 0, gradient, hessian)
    weights[...] = jnp.where(node[...] == node_q, values, 0.0).astype(BF16)
    local = feature[...] - feat_start
    diagonal = iota((NODES, NODES), 0) == iota((NODES, NODES), 1)
    local_n = jnp.sum(jnp.where(diagonal, local, 0), axis=1, keepdims=True)
    cut_n = jnp.sum(jnp.where(diagonal, cut[...], 0), axis=1, keepdims=True)
    owned_n = (local_n >= 0) & (local_n < FEATS)
    chooser = jnp.where(iota((NODES, FEATS), 1) == local_n, 1.0, 0.0).astype(BF16)
    split_values = jnp.dot(
        chooser, columns[...].astype(F32).astype(BF16), preferred_element_type=F32
    )
    hot = node[...] == iota((NODES, ROWS), 0)
    value = jnp.sum(jnp.where(hot, split_values, 0.0), axis=0, keepdims=True)
    owned = jnp.sum(jnp.where(hot & owned_n, 1.0, 0.0), axis=0, keepdims=True)
    row_cut = jnp.sum(jnp.where(hot, cut_n.astype(F32), 0.0), axis=0, keepdims=True)
    right = jnp.where(value > row_cut, owned, 0.0)
    chosen[...] = jnp.where(owned > 0.5, value, -1.0).astype(jnp.int32)
    sums = bin_sums(weights, lambda k: chosen[:, k * TILE : (k + 1) * TILE])
    sums = jnp.concatenate([sums[:64], sums[64:]], axis=1).astype(BF16).astype(F32)
    cut_q = jnp.sum(
        jnp.where(iota((2 * NODES, NODES), 1) == node_q, cut[...], 0), axis=1, keepdims=True
    )
    below = iota((2 * NODES, BINS), 1) <= cut_q
    left = jnp.sum(jnp.where(below, sums, 0.0), axis=1, keepdims=True)
    whole = jnp.sum(sums, axis=1, keepdims=True)
    lane = iota((2 * NODES, 128), 1)
    slot = 2 * node_q + channel
    entries = jnp.where(lane == slot, left, 0.0) + jnp.where(lane == slot + 64, whole, 0.0)
    half = ROWS // 2
    lines = [
        right[:, i * 128 : (i + 1) * 128] + 2.0 * right[:, half + i * 128 : half + (i + 1) * 128]
        for i in range(8)
    ]
    lines.append(jnp.sum(entries, axis=0, keepdims=True))
    for p in range(16):
        for i in range(9):
            pay[p, i] = lines[i]


def stage(columns, node, margin, labels, feature, cut):
    return pl.pallas_call(
        stage_kernel,
        out_shape=(
            pltpu.VMEM((2 * NODES, ROWS), BF16),
            pltpu.VMEM((16, 9, 1, 128), F32),
        ),
        in_specs=[VMEM] * 6,
        out_specs=[VMEM] * 2,
        scratch_shapes=[pltpu.VMEM((1, ROWS), jnp.int32)],
        name="stage",
        compiler_params=LIMIT,
        cost_estimate=cost(2 * 96 * ROWS * FEATS, 3 << 20),
    )(columns, node, margin, labels, feature, cut)


def histogram_kernel(first, count, weights, columns, send, keep):
    def feature(f, carry):
        sums = bin_sums(
            weights, lambda k: columns[pl.ds(first + f, 1), k * TILE : (k + 1) * TILE]
        ).astype(BF16)
        for h in range(2):
            span = slice(h * 128, (h + 1) * 128)
            send[f, :, span] = sums[64 * h : 64 * h + NODES]
            keep[f, :, span] = sums[64 * h + NODES : 64 * h + 64]
        return carry

    lax.fori_loop(0, count, feature, 0, unroll=count)


def histograms(weights, columns, first, count):
    half = pltpu.VMEM((count, NODES, BINS), BF16)
    return pl.pallas_call(
        functools.partial(histogram_kernel, first, count),
        out_shape=(half, half),
        in_specs=[VMEM] * 2,
        out_specs=[VMEM] * 2,
        compiler_params=LIMIT,
        cost_estimate=cost(2 * 64 * ROWS * count * BINS, 3 << 20),
    )(weights, columns)


def chip_sum_kernel(keep, arrived, sent, own, send):
    for f in range(0, keep.shape[0], 8):
        total = keep[f : f + 8].astype(F32) + arrived[f : f + 8].astype(F32)
        own[f : f + 8] = total[:, :16]
        send[f : f + 8] = total[:, 16:].astype(BF16)


def chip_sum(keep, arrived, sent):
    count = keep.shape[0]
    return pl.pallas_call(
        chip_sum_kernel,
        out_shape=(
            pltpu.VMEM((count, 16, BINS), F32),
            pltpu.VMEM((count, 16, BINS), BF16),
        ),
        in_specs=[VMEM, VMEM, pl.BlockSpec(memory_space=pl.ANY)],
        out_specs=[VMEM] * 2,
        name="chip_sum",
        compiler_params=LIMIT,
        cost_estimate=cost(count * 32 * BINS, 3 << 20),
    )(near(keep), near(arrived), near(sent))


def relay_kernel(line, sent, pay):
    here = lax.axis_index("zl") * 2 + lax.axis_index("core")
    for i in range(9):
        total = line[here, i] if i < 8 else line[0, i]
        for m in range(1, 4 if i < 8 else 16):
            total = total + (line[4 * m + here, i] if i < 8 else line[m, i])
        for p in range(32):
            pay[p, i] = total


def relay(line, sent):
    return pl.pallas_call(
        relay_kernel,
        out_shape=pltpu.VMEM((32, 9, 1, 128), F32),
        in_specs=[VMEM, pl.BlockSpec(memory_space=pl.ANY)],
        out_specs=VMEM,
        name="relay",
        compiler_params=LIMIT,
        cost_estimate=cost(32 * 9 * 128, 1 << 17),
    )(near(line), near(sent))


def finish_kernel(count, own, arrived, sent, *rest):
    histogram, total = rest[-2:]
    for f in range(0, count, 8):
        piece = (own[f : f + 8] + arrived[f : f + 8].astype(F32)).reshape(128, BINS)
        for h in range(2):
            total[h, f * 16 : (f + 8) * 16, :] = piece[:, h * 128 : (h + 1) * 128]
    for q in range(16):
        for h in range(2):
            histogram[q, :, h * 128 : (h + 1) * 128] = total[h, pl.ds(q, count, stride=16), :]


def finish(own, arrived, sent, first, so_far=None):
    count = own.shape[0]
    anywhere = pl.BlockSpec(memory_space=pl.ANY)
    more = () if so_far is None else (so_far,)
    return pl.pallas_call(
        functools.partial(finish_kernel, count),
        out_shape=jax.ShapeDtypeStruct((16, FEATS, BINS), F32),
        grid=(1,),
        in_specs=[VMEM, VMEM, anywhere] + [anywhere] * len(more),
        out_specs=pl.BlockSpec((16, count, BINS), lambda i: (0, first // count, 0)),
        scratch_shapes=[pltpu.VMEM((2, count * 16, 128), F32)],
        input_output_aliases={3: 0} if more else {},
        compiler_params=LIMIT,
        cost_estimate=cost(count * 16 * BINS, 3 << 20),
    )(near(own), near(arrived), near(sent), *more)


def rows_kernel(parts, node, margin, labels, sent, margin_out, child_out, grad_out, codes_ref):
    for i in range(8):
        line = parts[0, i]
        for p in range(1, 32):
            line = line + parts[p, i]
        codes_ref[i : i + 1, :] = line
    table = parts[0, 8]
    for p in range(1, 32):
        table = table + parts[p, 8]
    codes = codes_ref[...]
    table = jnp.broadcast_to(table, (8, 128))
    rest = pltpu.roll(table, 64, 1) - table
    leaf_left = -table / (pltpu.roll(table, 127, 1) + 1.0)
    leaf_right = -rest / (pltpu.roll(rest, 127, 1) + 1.0)
    high = jnp.where(codes > 1.5, 1.0, 0.0)
    go_right = jnp.concatenate([codes - 2.0 * high, high], axis=0) > 0.5
    node_here = node[...]
    shift = jnp.zeros((16, 128), F32)
    for n in range(NODES):
        step = jnp.where(
            go_right,
            jnp.broadcast_to(leaf_right[0:1, 2 * n : 2 * n + 1], (16, 128)),
            jnp.broadcast_to(leaf_left[0:1, 2 * n : 2 * n + 1], (16, 128)),
        )
        shift = jnp.where(node_here == n, step, shift)
    moved = margin[...] + shift
    margin_out[...] = moved
    child_out[...] = 2 * node_here + jnp.where(go_right, 1, 0)
    fresh = jax.nn.sigmoid(moved)
    slope = fresh - labels[...]
    curve = fresh * (1.0 - fresh)
    for i in range(16):
        grad_out[0:1, i * 128 : (i + 1) * 128] = slope[i : i + 1, :]
        grad_out[1:2, i * 128 : (i + 1) * 128] = curve[i : i + 1, :]


def rows_update(parts, node, margin, labels, sent):
    return pl.pallas_call(
        rows_kernel,
        out_shape=(
            jax.ShapeDtypeStruct((16, 128), F32),
            jax.ShapeDtypeStruct((16, 128), jnp.int32),
            jax.ShapeDtypeStruct((2, ROWS), F32),
        ),
        in_specs=[VMEM] * 4 + [pl.BlockSpec(memory_space=pl.ANY)],
        out_specs=[VMEM] * 3,
        scratch_shapes=[pltpu.VMEM((8, 128), F32)],
        name="rows_update",
        compiler_params=LIMIT,
        cost_estimate=cost(ROWS * 128, 1 << 17),
    )(parts, node, margin, labels, near(sent))


def share(spread, axes):
    return lax.all_to_all(spread, axes, 0, 0, tiled=True)


def on_device(binned, node_of, margin, labels, split_feature, split_bin):
    swap = [(0, 1), (1, 0)]
    columns = binned.T
    weights, pay = stage(
        far(columns),
        far(node_of.reshape(1, ROWS)),
        far(margin.reshape(1, ROWS)),
        far(labels.reshape(1, ROWS)),
        far(split_feature.reshape(1, NODES)),
        far(split_bin.reshape(1, NODES)),
    )
    line = share(pay, LINE)
    send_a, keep_a = histograms(near(weights), near(columns), 0, CUT)
    arrived_a = lax.ppermute(send_a, "core", swap)
    pay = relay(line, pay)
    parts = share(pay, PLANE)
    own_a, line_a = chip_sum(keep_a, arrived_a, send_a)
    arrived_a = lax.ppermute(line_a, "zl", swap)
    send_b, keep_b = histograms(near(weights), near(columns), CUT, FEATS - CUT)
    arrived_b = lax.ppermute(send_b, "core", swap)
    own_b, line_b = chip_sum(keep_b, arrived_b, send_b)
    arrived_b = lax.ppermute(line_b, "zl", swap)
    histogram = finish(own_a, arrived_a, line_a, 0)
    margin_out, child_out, grad_out = rows_update(
        near(parts),
        near(node_of.reshape(16, 128)),
        near(margin.reshape(16, 128)),
        near(labels.reshape(16, 128)),
        pay,
    )
    histogram = finish(own_b, arrived_b, line_b, CUT, histogram)
    return (
        histogram.reshape(8, 2, FEATS, BINS),
        margin_out.reshape(ROWS),
        child_out.reshape(ROWS),
        grad_out,
    )


def solution(mesh):
    fine = Mesh(mesh.devices.reshape(4, 8, 4, 2, 2), ("x", "y", "zh", "zl", "core"))
    rows = P(ROW_AXES)
    in_specs = (P(ROW_AXES, FEAT_AXES), rows, rows, rows, P(), P())
    out_specs = (P(ROW_AXES, None, FEAT_AXES, None), rows, rows, P(None, ROW_AXES))

    return jax.shard_map(
        on_device, mesh=fine, in_specs=in_specs, out_specs=out_specs, check_vma=False
    )
```
